32 devices in a mesh: seq: 16 (over z, y, x), head: 2 (over core).
Axes of the slice: x: 2, y: 2, z: 4, core: 2. Of those that a mesh axis runs over, the one named last changes fastest.
Arguments:
- queries: bfloat16 [12288, 128], P('seq'), may hold values from -6 to 6
- keys: bfloat16 [12288, 128], P('seq'), may hold values from -0.023925781 to 0.023925781
- values: bfloat16 [12288, 8192], P('seq', 'head'), may hold values from -6 to 6
- log_decay: float32 [128, 12288], P('head', 'seq'), may hold values from -0.8 to 0
- level_weight: bfloat16 [5, 128, 12288], P(None, 'head', 'seq'), may hold values from 0.099609375 to 1
- skip: float32 [128], P('head'), may hold values from 0.4 to 4.5
- norm_gain: bfloat16 [8192], P('head'), may hold values from 0.25 to 1.75
Outputs:
- normed: bfloat16 [12288, 8192], P('seq', 'head')
The draws below stay inside these ranges and needn't reach their ends.
All inputs are finite; a program needn't handle non-finite values.
Results may differ from the reference program's by a relative error of at most 0.007.
Values sent between devices are 32-bit elements; how exact they have to be, the bound alone decides.
No kernel may reach another device: no remote copies, remote signals or barrier semaphores. Data moves between devices by JAX's collectives and lax.ppermute only.
A program may use at most 192 MiB of HBM per device.

```python
import jax
import jax.numpy as jnp
from jax import lax

HEAD_COUNT = 128
HEAD_DIM = 64
STATE = 128
TOK_DEV = 768
TOKEN_COUNT = 12288
LEVELS = 4
N_SEQ = 16


def draw_log_decay(key, part):
    partition_random_key = jax.random.split(jax.random.fold_in(key, 11), 7)
    slow_share = 0.5
    slow_heads = jax.random.uniform(partition_random_key[0], (HEAD_COUNT,), jnp.float32) < slow_share
    fast_rate = jnp.exp(jax.random.uniform(partition_random_key[1], (HEAD_COUNT,), jnp.float32, jnp.log(1.0 / 50.0), jnp.log(1.0 / 30.0)))
    slow_rate = jnp.exp(jax.random.uniform(partition_random_key[2], (HEAD_COUNT,), jnp.float32, jnp.log(0.02), jnp.log(0.3))) / TOKEN_COUNT
    baseline_decay_rate = jnp.where(slow_heads, slow_rate, fast_rate)[:, None]
    block_multiplier = jax.random.uniform(partition_random_key[3], (HEAD_COUNT, TOKEN_COUNT // TOK_DEV), jnp.float32, 0.5, 1.5)
    block_multiplier = jnp.repeat(block_multiplier, TOK_DEV, axis=1)
    jitter_strength = jax.random.uniform(partition_random_key[4], (HEAD_COUNT, TOKEN_COUNT), jnp.float32, 0.5, 2.0)
    spike_positions = jax.random.randint(partition_random_key[5], (2,), 0, TOKEN_COUNT)
    position_list = jnp.arange(TOKEN_COUNT)
    spike_match = jnp.any(position_list[:, None] == spike_positions[None, :], axis=1)
    spike_penalty = jax.random.uniform(partition_random_key[6], (HEAD_COUNT,), jnp.float32, 0.2, 0.5)
    spike_component = jnp.where(spike_match[None, :], jnp.log(1.0 - spike_penalty)[:, None], 0.0)
    return (-baseline_decay_rate * block_multiplier * jitter_strength + spike_component).astype(jnp.float32)


def draw_skip(key, part):
    head_pos = jnp.arange(HEAD_COUNT, dtype=jnp.float32) / (HEAD_COUNT - 1)
    rough = jax.random.uniform(jax.random.fold_in(key, 29), (HEAD_COUNT,), jnp.float32, 0.5, 1.5)
    return ((1.0 + 2.0 * head_pos) * rough).astype(jnp.float32)


def levels(stream_key, dims, pieces, low, top_value):
    def one(axis_at, blocks):
        heights = jax.random.uniform(jax.random.fold_in(jax.random.fold_in(stream_key, 6), axis_at), (blocks,), jnp.float32, low / len(pieces), top_value / len(pieces))
        return jnp.repeat(jnp.exp(heights), dims[axis_at] // blocks).reshape((-1,) + (1,) * (len(dims) - axis_at - 1))

    gain = one(*pieces[0])
    for cut in pieces[1:]:
        gain = gain * one(*cut)
    return gain


def scatter_about(own_key, shape, deviation, limit, cuts=(), held_as=jnp.bfloat16):
    values = jax.random.normal(own_key, shape, jnp.float32) * deviation
    if len(cuts) > 0:
        values = levels(own_key, shape, cuts, -0.22, 0.18) * values
    return jnp.clip(values, min=-limit, max=limit).astype(held_as)


def setup_inputs(seed: int = 0) -> dict:
    arg_keys = jax.random.split(jax.random.key(seed), 8)
    queries = scatter_about(arg_keys[0], (TOKEN_COUNT, STATE), 1.0, 6.0, ((0, 16),))
    keys = scatter_about(arg_keys[1], (TOKEN_COUNT, STATE), 0.004, 0.023925781, ((0, 16),))
    values = scatter_about(arg_keys[2], (TOKEN_COUNT, HEAD_COUNT * HEAD_DIM), 1.0, 6.0, ((0, 16), (1, 2)))
    log_decay = draw_log_decay(jax.random.fold_in(arg_keys[7], 71), 0)
    level_weight = jnp.clip(0.099609375 + 0.9003906 * jax.random.uniform(arg_keys[4], (LEVELS + 1, HEAD_COUNT, TOKEN_COUNT), jnp.float32) ** levels(arg_keys[4], (LEVELS + 1, HEAD_COUNT, TOKEN_COUNT), ((1, 2), (2, 16)), -0.2, 0.2), 0.099609375, 1.0).astype(jnp.bfloat16)
    skip = draw_skip(jax.random.fold_in(arg_keys[7], 71), 0)
    norm_gain = jnp.clip(1.0 + 0.15 * jax.random.normal(arg_keys[6], (HEAD_COUNT * HEAD_DIM,), jnp.float32), 0.25, 1.75).astype(jnp.bfloat16)
    return {"queries": queries, "keys": keys, "values": values, "log_decay": log_decay, "level_weight": level_weight, "skip": skip, "norm_gain": norm_gain}


def reference(queries, keys, values, log_decay, level_weight, skip, norm_gain):
    blocks = N_SEQ
    span = TOK_DEV
    query_blk = queries.astype(jnp.float32).reshape(blocks, span, STATE)
    key_blk = keys.astype(jnp.float32).reshape(blocks, span, STATE)
    scores = jnp.einsum('dtn,dsn->dts', query_blk, key_blk)
    position = jnp.arange(span, dtype=jnp.int32)
    causal = position[:, None] >= position[None, :]
    head_vals = values.reshape(TOKEN_COUNT, HEAD_COUNT, HEAD_DIM).transpose(1, 0, 2)
    weights_all = level_weight.transpose(1, 0, 2)
    block_ids = jnp.arange(blocks, dtype=jnp.int32)

    def one_head(inputs):
        decay, head_in, lam, skip_one = inputs
        cum_decay = jnp.cumsum(decay.reshape(blocks, span), axis=1)
        vals_f32 = head_in.astype(jnp.float32).reshape(blocks, span, HEAD_DIM)
        lam_f32 = lam.astype(jnp.float32).reshape(LEVELS + 1, blocks, span)
        spread_in = jnp.where(causal[None], cum_decay[:, :, None] - cum_decay[:, None, :], jnp.float32(0.0))
        mixing = (jnp.where(causal[None], jnp.exp(spread_in), jnp.float32(0.0)) * scores).astype(jnp.bfloat16)
        mixing = lax.optimization_barrier(mixing).astype(jnp.float32)
        inner = jnp.einsum('dts,dsp->dtp', mixing, vals_f32)
        tail = jnp.exp(cum_decay[:, -1:] - cum_decay)
        scaled_keys = (key_blk * tail[:, :, None]).astype(jnp.bfloat16)
        scaled_keys = lax.optimization_barrier(scaled_keys).astype(jnp.float32)
        states = jnp.einsum('dsn,dsp->dnp', scaled_keys, vals_f32)
        result = lam_f32[0][:, :, None] * inner + skip_one * vals_f32
        prefix = jnp.concatenate([jnp.zeros((1,), jnp.float32), jnp.cumsum(cum_decay[:, -1])])
        for level_no in range(LEVELS):
            stride = 2 ** level_no
            upper = (block_ids - block_ids % stride).astype(jnp.int32)
            lower = (upper - stride).astype(jnp.int32)
            present = block_ids // stride % 2 == 1
            inside = (block_ids[None, :] >= lower[:, None]) & (block_ids[None, :] < upper[:, None]) & present[:, None]
            spread = jnp.where(inside, prefix[upper][:, None] - prefix[block_ids + 1][None, :], jnp.float32(0.0))
            mixer = jnp.where(inside, jnp.exp(spread), jnp.float32(0.0))
            bucket = jnp.einsum('de,enp->dnp', mixer, states, precision=lax.Precision.HIGHEST)
            gap = prefix[block_ids] - prefix[upper]
            present_f = jnp.where(present, jnp.float32(1.0), jnp.float32(0.0))
            coef = lam_f32[level_no + 1] * present_f[:, None] * jnp.exp(cum_decay + gap[:, None])
            cross = jnp.einsum('dtn,dnp->dtp', query_blk, bucket, precision=lax.Precision.HIGHEST)
            result = result + coef[:, :, None] * cross
        return result.reshape(TOKEN_COUNT, HEAD_DIM)
    mixed_out = lax.map(one_head, (log_decay, head_vals, weights_all, skip))
    squares = lax.optimization_barrier(jnp.sum(mixed_out * mixed_out, axis=(0, 2)))
    inv_rms = lax.rsqrt(squares / (HEAD_COUNT * HEAD_DIM) + 1e-05)
    scaled_out = mixed_out * inv_rms[None, :, None]
    result_all = scaled_out.transpose(1, 0, 2).reshape(TOKEN_COUNT, HEAD_COUNT * HEAD_DIM) * norm_gain.astype(jnp.float32)
    return result_all.astype(jnp.bfloat16)
```

```python
import functools

import jax
import jax.numpy as jnp
from jax import lax
from jax.experimental import pallas as pl
from jax.experimental.pallas import tpu as pltpu
from jax.sharding import PartitionSpec as P

F32 = jnp.float32
BF16 = jnp.bfloat16
SUB = 128
CHUNKS = 4
GROUP = 8


def dot(a, b, dims=((1,), (0,))):
    return lax.dot_general(a, b, (dims, ((), ())), preferred_element_type=F32)


def split3(x):
    hi = x.astype(BF16)
    r = x - hi.astype(F32)
    mid = r.astype(BF16)
    return hi, mid, (r - mid.astype(F32)).astype(BF16)


def factors_kernel(decay_ref, lw_ref, src_ref, dst_ref, tail_ref, grow_ref, fa_ref, fb_ref, tot_ref):
    heads, toks = decay_ref.shape
    row = lax.broadcasted_iota(jnp.int32, (SUB, SUB), 0)
    col = lax.broadcasted_iota(jnp.int32, (SUB, SUB), 1)
    tri = jnp.where(row <= col, 1.0, 0.0).astype(BF16)
    subs = toks // SUB
    base = jnp.zeros((heads, 1), F32)
    local = []
    for i in range(subs):
        at = pl.ds(i * SUB, SUB)
        hi, mid, lo = split3(decay_ref[:, at])
        cum = dot(hi, tri) + dot(mid, tri) + dot(lo, tri)
        middle = cum[:, SUB // 2 - 1 : SUB // 2]
        end = cum[:, SUB - 1 : SUB]
        src_ref[:, at] = jnp.exp(middle - cum)
        dst_ref[:, at] = jnp.exp(cum - middle) * lw_ref[0, :, :][:, i * SUB : (i + 1) * SUB].astype(F32)
        fa_ref[:, at] = jnp.broadcast_to(jnp.exp(end - middle), (heads, SUB))
        fb_ref[:, at] = jnp.broadcast_to(jnp.exp(middle), (heads, SUB))
        full = cum + base
        grow_ref[:, at] = jnp.exp(full)
        local.append(full)
        base = base + end
    for i in range(subs):
        tail_ref[:, pl.ds(i * SUB, SUB)] = jnp.exp(jnp.minimum(base - local[i], 0.0))
    tot_ref[...] = jnp.broadcast_to(base, (heads, SUB))


def make_factors(log_decay, level_weight):
    heads, toks = log_decay.shape
    big = jax.ShapeDtypeStruct((heads, toks), F32)
    return pl.pallas_call(
        factors_kernel,
        out_shape=(big, big, big, big, big, big, jax.ShapeDtypeStruct((heads, SUB), F32)),
        grid=(1,),
        in_specs=[
            pl.BlockSpec((heads, toks), lambda i: (0, 0)),
            pl.BlockSpec((1, heads, toks), lambda i: (0, 0, 0)),
        ],
        out_specs=tuple([pl.BlockSpec((heads, toks), lambda i: (0, 0))] * 6 + [pl.BlockSpec((heads, SUB), lambda i: (0, 0))]),
        name="factors",
    )(log_decay, level_weight)


def scale_heads(x_t, fac, size):
    g = fac.shape[0]
    return (x_t.reshape(g, size, x_t.shape[1]) * fac[:, None, :]).reshape(x_t.shape)


def state_kernel(size, v_ref, k_ref, tail_ref, s_ref):
    v_t = v_ref[...].T.astype(F32)
    scaled = scale_heads(v_t, tail_ref[...], size).astype(BF16)
    s_ref[...] = dot(scaled, k_ref[...])


def chunk_state(values, keys, tail, chunk, chunks, group):
    toks, width = values.shape
    heads = tail.shape[0]
    size = width // heads
    n = keys.shape[1]
    rows = group * size
    steps = heads // chunks // group
    first = chunk * steps
    return pl.pallas_call(
        functools.partial(state_kernel, size),
        out_shape=jax.ShapeDtypeStruct((steps * rows, n), F32),
        grid=(steps,),
        in_specs=[
            pl.BlockSpec((toks, rows), lambda i: (0, first + i)),
            pl.BlockSpec((toks, n), lambda i: (0, 0)),
            pl.BlockSpec((group, toks), lambda i: (first + i, 0)),
        ],
        out_specs=pl.BlockSpec((rows, n), lambda i: (i, 0)),
        cost_estimate=pl.CostEstimate(
            flops=2 * steps * rows * toks * n, bytes_accessed=2 * toks * steps * rows + 4 * steps * rows * n, transcendentals=0
        ),
        name="state",
    )(values, keys, tail)


def mix_kernel(size, levels, *refs):
    (v_ref, q_ref, k_ref, src_ref, dst_ref, fa_ref, fb_ref, coef_ref, skip_ref, gain_ref) = refs[:10]
    bucket_refs = refs[10 : 10 + levels]
    x_ref, sq_ref, qt_ref, mt_ref = refs[-4:]
    toks = v_ref.shape[0]
    rows = v_ref.shape[1]
    subs = toks // SUB
    step = pl.program_id(0)

    @pl.when(step == 0)
    def _():
        qt_ref[...] = q_ref[...].T
        row = lax.broadcasted_iota(jnp.int32, (SUB, SUB), 0)
        col = lax.broadcasted_iota(jnp.int32, (SUB, SUB), 1)
        for i in range(subs):
            at = pl.ds(i * SUB, SUB)
            sc = dot(k_ref[at, :], q_ref[at, :], ((1,), (1,)))
            mt_ref[:, at] = jnp.where(row <= col, sc, 0.0).astype(BF16)
        sq_ref[...] = jnp.zeros_like(sq_ref)

    v_t = v_ref[...].T.astype(F32)
    scaled = scale_heads(v_t, src_ref[...], size).astype(BF16)
    run = None
    inner = []
    for i in range(subs):
        cols = slice(i * SUB, (i + 1) * SUB)
        at = pl.ds(i * SUB, SUB)
        part = dot(scaled[:, cols], mt_ref[:, at])
        if i > 0:
            begin = scale_heads(run, fb_ref[:, at], size)
            part = part + dot(begin.astype(BF16), qt_ref[:, at])
        inner.append(part)
        if i < subs - 1:
            kv = dot(scaled[:, cols], k_ref[at, :])
            run = scale_heads(kv if i == 0 else begin + kv, fa_ref[:, at], size)
    x = scale_heads(jnp.concatenate(inner, axis=1), dst_ref[...], size)
    x = x + scale_heads(v_t, skip_ref[...], size)
    for l in range(levels):
        proj = dot(bucket_refs[l][...].astype(BF16), qt_ref[...])
        x = x + scale_heads(proj, coef_ref[l], size)
    sq = (x * x).reshape(rows // 8, 8, toks).sum(axis=0)
    sq_ref[...] += sq
    x_ref[...] = x * gain_ref[...][:, :1]


def chunk_mix(values, queries, keys, src, dst, fa, fb, coef, skip_b, gain_b, buckets, chunk, chunks, group):
    toks, width = values.shape
    heads = src.shape[0]
    size = width // heads
    n = keys.shape[1]
    rows = group * size
    steps = heads // chunks // group
    first = chunk * steps
    levels = len(buckets)
    whole = pl.BlockSpec((toks, n), lambda i: (0, 0))
    per_head = pl.BlockSpec((group, toks), lambda i: (first + i, 0))
    return pl.pallas_call(
        functools.partial(mix_kernel, size, levels),
        out_shape=(jax.ShapeDtypeStruct((steps * rows, toks), F32), jax.ShapeDtypeStruct((8, toks), F32)),
        grid=(steps,),
        in_specs=[
            pl.BlockSpec((toks, rows), lambda i: (0, first + i)),
            whole,
            whole,
            per_head,
            per_head,
            per_head,
            per_head,
            pl.BlockSpec((levels, group, toks), lambda i: (0, first + i, 0)),
            per_head,
            pl.BlockSpec((rows, SUB), lambda i: (first + i, 0)),
        ]
        + [pl.BlockSpec((rows, n), lambda i: (i, 0))] * levels,
        out_specs=(pl.BlockSpec((rows, toks), lambda i: (i, 0)), pl.BlockSpec((8, toks), lambda i: (0, 0))),
        scratch_shapes=[pltpu.VMEM((n, toks), BF16), pltpu.VMEM((SUB, toks), BF16)],
        cost_estimate=pl.CostEstimate(
            flops=2 * steps * rows * toks * n * (levels + 3), bytes_accessed=6 * toks * steps * rows, transcendentals=0
        ),
        name="mix",
    )(values, queries, keys, src, dst, fa, fb, coef, skip_b, gain_b, *buckets)


def norm_kernel(chunks, steps, inv_ref, *refs):
    x_refs, o_ref = refs[:chunks], refs[chunks]
    step = pl.program_id(0)
    for c in range(chunks):

        @pl.when(step // steps == c)
        def _():
            o_ref[...] = (x_refs[c][...] * inv_ref[...]).astype(BF16).T


def normalize(parts, inv_rms, rows):
    chunks = len(parts)
    chunk_rows, toks = parts[0].shape
    steps = chunk_rows // rows

    def pick(c):
        return lambda i: (jnp.clip(i - c * steps, 0, steps - 1), 0)

    return pl.pallas_call(
        functools.partial(norm_kernel, chunks, steps),
        out_shape=jax.ShapeDtypeStruct((toks, chunks * chunk_rows), BF16),
        grid=(chunks * steps,),
        in_specs=[pl.BlockSpec((1, toks), lambda i: (0, 0))] + [pl.BlockSpec((rows, toks), pick(c)) for c in range(chunks)],
        out_specs=pl.BlockSpec((toks, rows), lambda i: (0, i)),
        name="normalize",
    )(inv_rms, *parts)


def swap(value, axis, stride):
    return lax.ppermute(value, axis, [(i, i ^ (1 << stride)) for i in range(lax.axis_size(axis))])


def raise_up(value, axis, stride):
    half = 1 << stride
    return lax.ppermute(value, axis, [(i, i ^ half) for i in range(lax.axis_size(axis)) if not i & half])


def shards(queries, keys, values, log_decay, level_weight, skip, norm_gain):
    toks, width = values.shape
    heads = log_decay.shape[0]
    size = width // heads
    group = min(GROUP, heads)
    chunks = min(CHUNKS, heads // group)
    chunk_heads = heads // chunks
    levels = lax.axis_size("seq").bit_length() - 1
    index = lax.axis_index("seq")

    src, dst, tail, grow, fa, fb, tot = make_factors(log_decay, level_weight)

    group_total = tot[:, 0]
    offset = jnp.zeros_like(group_total)
    offsets, rights, flags = [], [], []
    for l in range(levels):
        bit = (index >> l) & 1
        other = swap(group_total, "seq", l)
        flags.append(bit == 1)
        offsets.append(jnp.where(bit == 1, jnp.exp(offset), 0.0))
        rights.append(jnp.exp(jnp.where(bit == 1, group_total, other)))
        offset = offset + jnp.where(bit == 1, other, 0.0)
        group_total = group_total + other
    coef = level_weight[1:].astype(F32) * grow[None] * jnp.stack(offsets)[:, :, None]

    skip_b = jnp.broadcast_to(skip[:, None], (heads, toks))
    gain_b = jnp.broadcast_to(norm_gain.astype(F32)[:, None], (width, SUB))

    states = [chunk_state(values, keys, tail, c, chunks, group) for c in range(chunks)]
    parts, squares = [], []
    for c in range(chunks):
        here = slice(c * chunk_heads, (c + 1) * chunk_heads)
        state = states[c]
        buckets = []
        for l in range(levels):
            if l + 1 < levels:
                got = swap(state, "seq", l)
                left = jnp.where(flags[l], got, state)
                right = jnp.where(flags[l], state, got)
                fac = jnp.repeat(rights[l][here], size)[:, None]
                state = fac * left + right
            else:
                got = raise_up(state, "seq", l)
            buckets.append(got)
        part, sq = chunk_mix(
            values, queries, keys, src, dst, fa, fb, coef, skip_b, gain_b, buckets, c, chunks, group
        )
        parts.append(part)
        squares.append(sq)
    sq = functools.reduce(jnp.add, squares).sum(axis=0)
    count = lax.axis_size("head")
    total = sq
    if count == 2:
        total = sq + lax.ppermute(sq, "head", [(0, 1), (1, 0)])
    else:
        total = lax.psum(sq, "head")
    inv_rms = lax.rsqrt(total / (width * count) + 1e-05)
    return normalize(parts, inv_rms[None, :], group * size)


def solution(mesh):
    placed = (
        P("seq", None),
        P("seq", None),
        P("seq", "head"),
        P("head", "seq"),
        P(None, "head", "seq"),
        P("head"),
        P("head"),
    )
    return jax.shard_map(
        shards, mesh=mesh, in_specs=placed, out_specs=P("seq", "head"), check_vma=False
    )
```
